32 devices in a mesh: ctx: 16 (over z, y, core), head: 2 (over x).
Axes of the slice: x: 2, y: 2, z: 4, core: 2. Of those that a mesh axis runs over, the one named last changes fastest.
Arguments:
- queries: bfloat16 [4096, 2048], P(('ctx', 'head')), may hold values from -200 to 200
- keys: bfloat16 [4096, 256], P(('ctx', 'head')), may hold values from -7 to 7
- values: bfloat16 [4096, 256], P(('ctx', 'head')), may hold values from -6 to 6
- output_cotangent: bfloat16 [4096, 2048], P(('ctx', 'head')), may hold values from -6 to 6
- doc_ids: int32 [4096], replicated, may hold values from 0 to 3, never falling along the last dimension, each value on 1 to 2048 neighbouring positions
Outputs:
- grad_queries: bfloat16 [4096, 2048], P(('ctx', 'head'))
- key_gradients: bfloat16 [4096, 256], P(('ctx', 'head'))
- value_gradients: bfloat16 [4096, 256], P(('ctx', 'head'))
The draws below stay inside these ranges and needn't reach their ends.
Inputs may be any that keep to these rules, and one draw needn't show every extreme that they name: `doc_ids`: document numbers never fall along the tokens; every number occurs; each document has 1 to 2048 tokens and one has exactly 2048.
All inputs are finite; a program needn't handle non-finite values.
Results may differ from the reference program's by a relative error of at most 0.017.
Values may be sent and summed in bfloat16 or wider, within the bound.
A program may use at most 128 MiB of HBM per device.

```python
import math
import jax
import jax.numpy as jnp
import numpy as np
from jax import lax

HEAD_DIMENSION = 128
QUERY_GROUP = 8
TOK_DEV = 256
MOST_DOC = 2048
KEY_VALUE_HEADS = 2
HQ = 16
TOTAL_TOKENS = 4096
DOCS = 4
SPAN = 8


def drawn_keys(key):
    key_initial = jnp.clip(jax.random.normal(jax.random.fold_in(key, 101), (TOTAL_TOKENS, KEY_VALUE_HEADS * HEAD_DIMENSION), jnp.float32), -6.0, 6.0)
    return key_initial


def draw_keys(key, part):
    key_initial = drawn_keys(key)
    return key_initial.astype(jnp.bfloat16)


def draw_queries(key, part):
    unmasked_rows = jnp.clip(jax.random.normal(jax.random.fold_in(key, 105), (TOTAL_TOKENS, KEY_VALUE_HEADS, QUERY_GROUP, HEAD_DIMENSION), jnp.float32), -6.0, 6.0)
    return unmasked_rows.reshape(TOTAL_TOKENS, HQ * HEAD_DIMENSION).astype(jnp.bfloat16)


def levels(stream_key, extent, pieces, least, top_value):
    def one(dim, parts):
        steps = jax.random.uniform(jax.random.fold_in(jax.random.fold_in(stream_key, 6), dim), (parts,), jnp.float32, least / len(pieces), top_value / len(pieces))
        return jnp.repeat(jnp.exp(steps), extent[dim] // parts).reshape((-1,) + (1,) * (len(extent) - dim - 1))

    factor_of = one(*pieces[0])
    for cut in pieces[1:]:
        factor_of = factor_of * one(*cut)
    return factor_of


def split_up(amount, total, limit, lean):
    portions = [(1 << 20) // math.isqrt(grade ** lean) + 1 for grade in range(2, amount + 1)]
    rest, counts = total - limit - (amount - 1), [1] * (amount - 1)
    while rest > 0:
        candidates = [i for i in range(amount - 1) if counts[i] < limit]
        whole, budget = sum([portions[i] for i in candidates]), rest
        for i in candidates:
            extra = min(limit - counts[i], max(1, budget * portions[i] // whole), rest)
            counts[i] = counts[i] + extra
            rest = rest - extra
    return np.array([limit] + counts)


def ragged(stream_key, count, total, bound, slope):
    if count == 2:
        one = jax.random.randint(stream_key, (), max(1, total - bound), min(bound, total - 1) + 1)
        return jnp.stack([one, total - one])
    lengths = jnp.asarray(split_up(count, total, bound, slope), jnp.int32)
    twos = (count - 1) // 2
    donor, sink = lengths[1:1 + 2 * twos:2], lengths[2:2 + 2 * twos:2]
    margin = jnp.minimum(donor - 1, bound - sink)
    moved = jax.random.randint(jax.random.fold_in(stream_key, 1), (twos,), 0, 1 << 20) % (margin + 1)
    lengths = lengths.at[1:1 + 2 * twos:2].set(donor - moved).at[2:2 + 2 * twos:2].set(sink + moved)
    return lengths[jax.random.permutation(jax.random.fold_in(stream_key, 2), count)]


def bell_draw(key, shape, scale, limit, split=(), kind=jnp.bfloat16):
    array = scale * jax.random.normal(key, shape, jnp.float32)
    if split:
        array = array * levels(key, shape, split, -0.22, 0.18)
    return jnp.clip(array, -limit, limit).astype(kind)


def setup_inputs(seed: int = 0) -> dict:
    arg_keys = jax.random.split(jax.random.key(seed), 6)
    return {
        "queries": draw_queries(jax.random.fold_in(arg_keys[5], 71), 0),
        "keys": draw_keys(jax.random.fold_in(arg_keys[5], 71), 0),
        "values": bell_draw(arg_keys[2], (TOTAL_TOKENS, KEY_VALUE_HEADS * HEAD_DIMENSION), 1.0, 6.0, ((0, 32),)),
        "output_cotangent": bell_draw(arg_keys[3], (TOTAL_TOKENS, HQ * HEAD_DIMENSION), 1.0, 6.0, ((0, 32),)),
        "doc_ids": jnp.searchsorted(jnp.cumsum(ragged(arg_keys[4], DOCS, TOTAL_TOKENS, MOST_DOC, 2)), jnp.arange(TOTAL_TOKENS), side="right").astype(jnp.int32),
    }


masked_score = -1.0e30


def reference(queries, keys, values, output_cotangent, doc_ids):
    scaling = HEAD_DIMENSION ** -0.5
    error_tolerance = SPAN * TOK_DEV
    window_len = error_tolerance + TOK_DEV
    query_entire = queries.reshape(TOTAL_TOKENS, KEY_VALUE_HEADS, QUERY_GROUP, HEAD_DIMENSION)
    gradient_total = output_cotangent.reshape(TOTAL_TOKENS, KEY_VALUE_HEADS, QUERY_GROUP, HEAD_DIMENSION)
    padded_key = jnp.concatenate([jnp.zeros((error_tolerance, KEY_VALUE_HEADS, HEAD_DIMENSION), keys.dtype), keys.reshape(TOTAL_TOKENS, KEY_VALUE_HEADS, HEAD_DIMENSION)], axis=0)
    padded_value = jnp.concatenate([jnp.zeros((error_tolerance, KEY_VALUE_HEADS, HEAD_DIMENSION), values.dtype), values.reshape(TOTAL_TOKENS, KEY_VALUE_HEADS, HEAD_DIMENSION)], axis=0)
    doc_all = doc_ids.astype(jnp.int32)
    doc_pad = jnp.concatenate([jnp.full((error_tolerance,), -1, jnp.int32), doc_all], axis=0)

    def one_block(carried, block_index):
        gradient_key, gradient_value = carried
        first_row = (block_index * TOK_DEV).astype(jnp.int32)
        query_blk = lax.dynamic_slice_in_dim(query_entire, first_row, TOK_DEV, 0).astype(jnp.float32)
        grad_blk = lax.dynamic_slice_in_dim(gradient_total, first_row, TOK_DEV, 0).astype(jnp.float32)
        key_blk = lax.dynamic_slice_in_dim(padded_key, first_row, window_len, 0).astype(jnp.float32)
        value_blk = lax.dynamic_slice_in_dim(padded_value, first_row, window_len, 0).astype(jnp.float32)
        query_docs = lax.dynamic_slice_in_dim(doc_all, first_row, TOK_DEV, 0)
        key_docs = lax.dynamic_slice_in_dim(doc_pad, first_row, window_len, 0)
        query_pos = jnp.arange(TOK_DEV, dtype=jnp.int32)[:, None] + error_tolerance
        key_pos = jnp.arange(window_len, dtype=jnp.int32)[None, :]
        allowed = (query_docs[:, None] == key_docs[None, :]) & (key_pos <= query_pos)
        scores = jnp.einsum("qhgd,khd->hgqk", query_blk, key_blk) * scaling
        masked = jnp.where(allowed, scores, masked_score)
        row_max = jnp.max(masked, axis=3)
        log_norm = row_max + jnp.log(jnp.sum(jnp.exp(masked - row_max[..., None]), axis=3))
        weights = jnp.where(allowed, jnp.exp(scores - log_norm[..., None]), 0.0)
        rounded = lax.optimization_barrier(weights.astype(jnp.bfloat16)).astype(jnp.float32)
        attn_out = jnp.einsum("hgqk,khd->qhgd", rounded, value_blk)
        row_dot = jnp.einsum("qhgd,qhgd->hgq", grad_blk, attn_out)
        grad_weights = jnp.einsum("qhgd,khd->hgqk", grad_blk, value_blk)
        grad_scores = (weights * (grad_weights - row_dot[..., None])).astype(jnp.bfloat16)
        grad_scores = lax.optimization_barrier(grad_scores).astype(jnp.float32)
        query_grad = jnp.einsum("hgqk,khd->qhgd", grad_scores, key_blk) * scaling
        key_part = jnp.einsum("hgqk,qhgd->khd", grad_scores, query_blk) * scaling
        value_part = jnp.einsum("hgqk,qhgd->khd", rounded, grad_blk)
        gradient_key = lax.dynamic_update_slice_in_dim(
            gradient_key, lax.dynamic_slice_in_dim(gradient_key, first_row, window_len, 0) + key_part, first_row, 0)
        gradient_value = lax.dynamic_update_slice_in_dim(
            gradient_value, lax.dynamic_slice_in_dim(gradient_value, first_row, window_len, 0) + value_part, first_row, 0)
        return (gradient_key, gradient_value), query_grad.astype(jnp.bfloat16)

    blank_gradient = jnp.zeros((error_tolerance + TOTAL_TOKENS, KEY_VALUE_HEADS, HEAD_DIMENSION), jnp.float32)
    (gradient_key, gradient_value), query_grads = lax.scan(
        one_block, (blank_gradient, blank_gradient), jnp.arange(TOTAL_TOKENS // TOK_DEV, dtype=jnp.int32))
    grad_queries = query_grads.reshape(TOTAL_TOKENS, HQ * HEAD_DIMENSION)
    key_gradients = gradient_key[error_tolerance:].astype(jnp.bfloat16).reshape(TOTAL_TOKENS, KEY_VALUE_HEADS * HEAD_DIMENSION)
    value_gradients = gradient_value[error_tolerance:].astype(jnp.bfloat16).reshape(TOTAL_TOKENS, KEY_VALUE_HEADS * HEAD_DIMENSION)
    return (grad_queries, key_gradients, value_gradients)
```

```python
import functools
import math

import jax
import jax.numpy as jnp
from jax import lax
from jax.experimental import pallas as pl
from jax.experimental.pallas import tpu as pltpu
from jax.sharding import PartitionSpec as P

SPAN = 8


masked_score = -1e30
LOG2E = math.log2(math.e)


def shifted(value, axis, steps):
    count = lax.axis_size(axis)
    leading, last = (max(0, -steps), min(count, count - steps))
    return lax.ppermute(value, axis, [(source, source + steps) for source in range(leading, last)])


def block_docs(doc_ids, block, length):
    block_count = doc_ids.shape[0] // length
    first_row = jnp.clip(block, 0, block_count - 1) * length
    return lax.dynamic_slice_in_dim(doc_ids, first_row, length, 0)


def attention_kernel(
    query_ref, grad_ref, key_ref, value_ref, bound_ref, dq_ref, dk_ref, dv_ref, bias_ref, key_t_ref, value_t_ref,
    *, scaling
):
    window, width = key_ref.shape
    length = query_ref.shape[0]
    group_size = query_ref.shape[1] // width
    own_block = lax.axis_index("ctx")
    key_row = lax.broadcasted_iota(jnp.int32, (window, length), 0)
    key_pos = (own_block - key_row // length) * length + key_row % length
    query_pos = own_block * length + lax.broadcasted_iota(jnp.int32, (1, length), 1)
    allowed = (key_pos >= bound_ref[...]) & (key_pos <= query_pos)
    bias_ref[...] = jnp.where(allowed, 0.0, masked_score)
    key_t_ref[...] = key_ref[...].T
    value_t_ref[...] = value_ref[...].T
    dk_ref[...] = jnp.zeros_like(dk_ref)
    dv_ref[...] = jnp.zeros_like(dv_ref)
    contract_last = (((1,), (1,)), ((), ()))

    @pl.loop(0, group_size)
    def _(g):
        cols = pl.ds(pl.multiple_of(g * width, width), width)
        query = query_ref[:, cols]
        grad = grad_ref[:, cols]
        scores = lax.dot_general(key_ref[...], query, contract_last, preferred_element_type=jnp.float32)
        scores = scores * (scaling * LOG2E) + bias_ref[...]
        powers = jnp.exp2(scores - jnp.max(scores, axis=0, keepdims=True))
        weights = powers * (1.0 / jnp.sum(powers, axis=0, keepdims=True))
        rounded = weights.astype(jnp.bfloat16)
        out_t = jnp.dot(value_t_ref[...], rounded, preferred_element_type=jnp.float32)
        row_dot = jnp.sum(grad.astype(jnp.float32).T * out_t, axis=0, keepdims=True)
        grad_weights = lax.dot_general(value_ref[...], grad, contract_last, preferred_element_type=jnp.float32)
        grad_scores = (weights * (grad_weights - row_dot)).astype(jnp.bfloat16)
        dq_t = jnp.dot(key_t_ref[...], grad_scores, preferred_element_type=jnp.float32)
        dq_ref[:, cols] = (dq_t * scaling).T.astype(jnp.bfloat16)
        dk_ref[...] += jnp.dot(grad_scores, query, preferred_element_type=jnp.float32)
        dv_ref[...] += jnp.dot(rounded, grad, preferred_element_type=jnp.float32)

    dk_ref[...] = dk_ref[...] * scaling


def attention(query_rows, grad_rows, key_window, value_window, bound):
    length = query_rows.shape[0]
    window, width = key_window.shape
    vmem = pl.BlockSpec(memory_space=pltpu.VMEM)
    return pl.pallas_call(
        functools.partial(attention_kernel, scaling=width ** (-0.5)),
        out_shape=(
            jax.ShapeDtypeStruct(query_rows.shape, jnp.bfloat16),
            jax.ShapeDtypeStruct((window, width), jnp.float32),
            jax.ShapeDtypeStruct((window, width), jnp.float32),
        ),
        in_specs=[vmem] * 5,
        out_specs=(vmem,) * 3,
        scratch_shapes=[
            pltpu.VMEM((window, length), jnp.float32),
            pltpu.VMEM((width, window), jnp.bfloat16),
            pltpu.VMEM((width, window), jnp.bfloat16),
        ],
        compiler_params=pltpu.CompilerParams(vmem_limit_bytes=56 * 1024 * 1024),
    )(query_rows, grad_rows, key_window, value_window, bound)


def on_device(queries, keys, values, output_cotangent, doc_ids):
    query_rows, grad_rows, key_rows, value_rows = (
        lax.all_to_all(queries, "head", split_axis=1, concat_axis=0, tiled=True),
        lax.all_to_all(output_cotangent, "head", split_axis=1, concat_axis=0, tiled=True),
        lax.all_to_all(keys, "head", split_axis=1, concat_axis=0, tiled=True),
        lax.all_to_all(values, "head", split_axis=1, concat_axis=0, tiled=True),
    )
    length = key_rows.shape[0]
    head_width = key_rows.shape[1]
    own_block = lax.axis_index("ctx")
    key_window = key_rows[None]
    value_window = value_rows[None]
    for level_index in range(SPAN.bit_length() - 1):
        stride = 2**level_index
        got_keys, got_values = shifted((key_window, value_window), "ctx", stride)
        key_window = jnp.concatenate([key_window, got_keys], axis=0)
        value_window = jnp.concatenate([value_window, got_values], axis=0)
    last_keys, last_values = shifted((key_rows, value_rows), "ctx", SPAN)
    key_window = jnp.concatenate([key_window, last_keys[None]], axis=0)
    value_window = jnp.concatenate([value_window, last_values[None]], axis=0)

    own_docs = block_docs(doc_ids, own_block, length)
    bound = jnp.sum((doc_ids[:, None] < own_docs[None, :]).astype(jnp.int32), axis=0)[None]
    near_reach = SPAN
    grad_query_out, part_keys, part_values = attention(
        query_rows,
        grad_rows,
        key_window.reshape(-1, head_width),
        value_window.reshape(-1, head_width),
        bound,
    )
    part_keys = part_keys.reshape(near_reach + 1, length, head_width)
    part_values = part_values.reshape(near_reach + 1, length, head_width)
    extra_zero = jnp.zeros((length, head_width), jnp.float32)
    extra_keys = extra_zero
    extra_values = extra_zero
    stack_len = max(near_reach, 1)
    stacked_keys = part_keys[:stack_len]
    stacked_values = part_values[:stack_len]
    back_keys, back_values = (
        shifted(part_keys[near_reach].astype(jnp.bfloat16), "ctx", -near_reach).astype(jnp.float32),
        shifted(part_values[near_reach].astype(jnp.bfloat16), "ctx", -near_reach).astype(
            jnp.float32
        ),
    )
    extra_keys = extra_keys + back_keys
    extra_values = extra_values + back_values
    for level_index in range(stack_len.bit_length() - 1):
        stride = stack_len // 2 ** (level_index + 1)
        back_keys, back_values = shifted(
            (stacked_keys[stride : 2 * stride], stacked_values[stride : 2 * stride]), "ctx", -stride
        )
        stacked_keys = stacked_keys[:stride] + back_keys
        stacked_values = stacked_values[:stride] + back_values
    key_total = stacked_keys[0]
    value_total = stacked_values[0]
    key_total = key_total + extra_keys
    value_total = value_total + extra_values
    grad_key_out = key_total.astype(jnp.bfloat16)
    grad_value_out = value_total.astype(jnp.bfloat16)
    out_queries, out_keys, out_values = (
        lax.all_to_all(grad_query_out, "head", split_axis=0, concat_axis=1, tiled=True),
        lax.all_to_all(grad_key_out, "head", split_axis=0, concat_axis=1, tiled=True),
        lax.all_to_all(grad_value_out, "head", split_axis=0, concat_axis=1, tiled=True),
    )
    return (out_queries, out_keys, out_values)


def solution(mesh):
    in_specs = (
        P(("ctx", "head"), None),
        P(("ctx", "head"), None),
        P(("ctx", "head"), None),
        P(("ctx", "head"), None),
        P(),
    )
    out_specs = (P(("ctx", "head"), None), P(("ctx", "head"), None), P(("ctx", "head"), None))
    return jax.shard_map(
        on_device, mesh=mesh, in_specs=in_specs, out_specs=out_specs, check_vma=False
    )
```

```python
import functools
import math

import jax
import jax.numpy as jnp
from jax import lax
from jax.experimental import pallas as pl
from jax.experimental.pallas import tpu as pltpu
from jax.sharding import PartitionSpec as P

SPAN = 8
PLANE = SPAN // 2
SLOTS = SPAN + PLANE

masked_score = -1e30
LOG2E = math.log2(math.e)
VMEM_LIMIT = 56 * 1024 * 1024
MESH = pl.DeviceIdType.MESH


def greet(partners):
    barrier = pltpu.get_barrier_semaphore()
    for partner in partners:
        pl.semaphore_signal(barrier, inc=1, device_id=partner, device_id_type=MESH)
    pl.semaphore_wait(barrier, len(partners))


def places():
    ctx, head = lax.axis_index("ctx"), lax.axis_index("head")
    count = lax.axis_size("ctx")
    slot = lax.rem(ctx, PLANE)
    base = ctx - slot
    up = lax.rem(ctx + PLANE, count)
    down = lax.rem(ctx + count - PLANE, count)
    far = lax.rem(slot + PLANE // 2, PLANE)
    near = slot + 1 - 2 * lax.rem(slot, 2)
    diagonal = lax.rem(near + PLANE // 2, PLANE)
    return ctx, head, slot, base, up, down, near, far, diagonal


def head_peers(head):
    count = lax.axis_size("head")
    return [lax.rem(head + step, count) for step in range(1, count)]


def rows_of(index, length):
    return pl.ds(pl.multiple_of(index * length, length), length)


def gather_kernel(
    query_ref, grad_ref, key_ref, value_ref, query_out, grad_out, key_out, value_out, local_sems, x_send, x_recv, c_send, c_recv
):
    ctx, head, slot, base, up, down, near, far, diagonal = places()
    peers = head_peers(head)
    tokens = key_ref.shape[0]
    length = tokens * lax.axis_size("head")
    pairs = [
        (key_ref, key_out, slot + SPAN),
        (value_ref, value_out, slot + SPAN),
        (query_ref, query_out, 0),
        (grad_ref, grad_out, 0),
    ]
    greet(
        [{"head": peer} for peer in peers]
        + [{"ctx": up}, {"ctx": down}, {"ctx": base + near}, {"ctx": base + far}]
    )
    x_copies = []
    for index, (source, target, block) in enumerate(pairs):
        width = target.shape[1]
        start = pl.multiple_of(block * length + head * tokens, tokens)
        copies = []
        for step, peer in enumerate(peers):
            copy = pltpu.make_async_remote_copy(
                src_ref=source.at[:, rows_of(peer, width)],
                dst_ref=target.at[pl.ds(start, tokens), :],
                send_sem=x_send.at[index, step],
                recv_sem=x_recv.at[index, step],
                device_id={"head": peer},
                device_id_type=MESH,
            )
            copy.start()
            copies.append(copy)
        local = pltpu.make_async_copy(
            source.at[:, rows_of(head, width)], target.at[pl.ds(start, tokens), :], local_sems.at[index]
        )
        local.start()
        x_copies.append((local, copies))

    def arrive(index):
        local, copies = x_copies[index]
        local.wait()
        for copy in copies:
            copy.wait_recv()

    def push(array, kind, level, block, partner):
        target = (key_out, value_out)[array]
        rows = rows_of((2 - level) * PLANE + block, length)
        copy = pltpu.make_async_remote_copy(
            src_ref=target.at[rows, :],
            dst_ref=target.at[rows, :]
            if kind
            else target.at[rows_of((1 - level) * PLANE + block, length), :],
            send_sem=c_send.at[array, kind, level],
            recv_sem=c_recv.at[array, kind, level],
            device_id={"ctx": partner},
            device_id_type=MESH,
        )
        copy.start()
        copies[array, kind, level] = copy

    copies = {}

    def spread(array, level):
        if level < 2:
            push(array, 0, level, slot, up)
        push(array, 1, level, slot, base + far)
        push(array, 2, level, slot, base + near)

    def relay(array, level):
        copies[array, 1, level].wait_recv()
        push(array, 3, level, far, base + near)

    for array in range(2):
        arrive(array)
        spread(array, 0)
    for array in range(2):
        copies[array, 0, 0].wait_recv()
        spread(array, 1)
    for array in range(2):
        relay(array, 0)
    for array in range(2):
        copies[array, 0, 1].wait_recv()
        spread(array, 2)
    for level in (1, 2):
        for array in range(2):
            relay(array, level)
    for array in range(2):
        for level in range(3):
            copies[array, 2, level].wait_recv()
            copies[array, 3, level].wait_recv()
    arrive(2)
    arrive(3)
    for _, remote in x_copies:
        for copy in remote:
            copy.wait_send()
    for copy in copies.values():
        copy.wait_send()


def gather(queries, output_cotangent, keys, values):
    heads = lax.axis_size("head")
    tokens, width = queries.shape
    length = tokens * heads
    head_width = keys.shape[1] // heads
    vmem = pl.BlockSpec(memory_space=pltpu.VMEM)
    rows = jax.ShapeDtypeStruct((length, width // heads), jnp.bfloat16)
    window = jax.ShapeDtypeStruct((SLOTS * length, head_width), jnp.bfloat16)
    dma = pltpu.SemaphoreType.DMA
    return pl.pallas_call(
        gather_kernel,
        out_shape=(rows, rows, window, window),
        in_specs=[vmem] * 4,
        out_specs=(vmem,) * 4,
        scratch_shapes=[dma((4,)), dma((4, heads)), dma((4, heads)), dma((2, 4, 3)), dma((2, 4, 3))],
        compiler_params=pltpu.CompilerParams(
            collective_id=0, has_side_effects=True, vmem_limit_bytes=VMEM_LIMIT
        ),
    )(queries, output_cotangent, keys, values)


def attention_kernel(
    query_ref, grad_ref, key_ref, value_ref, bound_ref, dq_ref, dk_ref, dv_ref,
    bias_ref, key_t_ref, value_t_ref, key_sum, value_sum, *, scaling
):
    length = query_ref.shape[0]
    width = key_ref.shape[1]
    window = key_sum.shape[0]
    group_size = query_ref.shape[1] // width
    own_block = lax.axis_index("ctx")
    slot = lax.rem(own_block, PLANE)
    reach = pl.ds(pl.multiple_of(slot * length, length), window)
    key_pos = (own_block - SPAN) * length + lax.broadcasted_iota(jnp.int32, (window, length), 0)
    query_pos = own_block * length + lax.broadcasted_iota(jnp.int32, (1, length), 1)
    allowed = (key_pos >= bound_ref[...]) & (key_pos <= query_pos)
    bias_ref[...] = jnp.where(allowed, 0.0, masked_score)
    key_t_ref[...] = key_ref[reach, :].T
    value_t_ref[...] = value_ref[reach, :].T
    key_sum[...] = jnp.zeros_like(key_sum)
    value_sum[...] = jnp.zeros_like(value_sum)
    contract_last = (((1,), (1,)), ((), ()))

    @pl.loop(0, group_size)
    def _(g):
        cols = pl.ds(pl.multiple_of(g * width, width), width)
        query = query_ref[:, cols]
        grad = grad_ref[:, cols]
        scores = lax.dot_general(key_ref[reach, :], query, contract_last, preferred_element_type=jnp.float32)
        scores = scores * (scaling * LOG2E) + bias_ref[...]
        powers = jnp.exp2(scores - jnp.max(scores, axis=0, keepdims=True))
        weights = powers * (1.0 / jnp.sum(powers, axis=0, keepdims=True))
        rounded = weights.astype(jnp.bfloat16)
        out_t = jnp.dot(value_t_ref[...], rounded, preferred_element_type=jnp.float32)
        row_dot = jnp.sum(grad.astype(jnp.float32).T * out_t, axis=0, keepdims=True)
        grad_weights = lax.dot_general(value_ref[reach, :], grad, contract_last, preferred_element_type=jnp.float32)
        grad_scores = (weights * (grad_weights - row_dot)).astype(jnp.bfloat16)
        dq_t = jnp.dot(key_t_ref[...], grad_scores, preferred_element_type=jnp.float32)
        dq_ref[:, cols] = (dq_t * scaling).T.astype(jnp.bfloat16)
        key_sum[...] += jnp.dot(grad_scores, query, preferred_element_type=jnp.float32)
        value_sum[...] += jnp.dot(rounded, grad, preferred_element_type=jnp.float32)

    dk_ref[...] = jnp.zeros_like(dk_ref)
    dv_ref[...] = jnp.zeros_like(dv_ref)
    dk_ref[reach, :] = (key_sum[...] * scaling).astype(jnp.bfloat16)
    dv_ref[reach, :] = value_sum[...].astype(jnp.bfloat16)


def attention(query_rows, grad_rows, key_window, value_window, bound):
    length = query_rows.shape[0]
    width = key_window.shape[1]
    window = (SPAN + 1) * length
    vmem = pl.BlockSpec(memory_space=pltpu.VMEM)
    parts = jax.ShapeDtypeStruct(key_window.shape, jnp.bfloat16)
    return pl.pallas_call(
        functools.partial(attention_kernel, scaling=width ** (-0.5)),
        out_shape=(jax.ShapeDtypeStruct(query_rows.shape, jnp.bfloat16), parts, parts),
        in_specs=[vmem] * 5,
        out_specs=(vmem,) * 3,
        scratch_shapes=[
            pltpu.VMEM((window, length), jnp.float32),
            pltpu.VMEM((width, window), jnp.bfloat16),
            pltpu.VMEM((width, window), jnp.bfloat16),
            pltpu.VMEM((window, width), jnp.float32),
            pltpu.VMEM((window, width), jnp.float32),
        ],
        compiler_params=pltpu.CompilerParams(vmem_limit_bytes=VMEM_LIMIT),
    )(query_rows, grad_rows, key_window, value_window, bound)


def reduce_kernel(
    dq_ref, dk_ref, dv_ref, dq_out, dk_out, dv_out,
    near_buf, own_sum, far_sum, far_buf, down_src, down_buf, final,
    local_sems, x_send, x_recv, c_send, c_recv
):
    ctx, head, slot, base, up, down, near, far, diagonal = places()
    peers = head_peers(head)
    tokens = dq_out.shape[0]
    length = dq_ref.shape[0]
    parts = (dk_ref, dv_ref)
    greet(
        [{"head": peer} for peer in peers]
        + [{"ctx": up}, {"ctx": down}, {"ctx": base + near}, {"ctx": base + far}]
    )
    waits = []

    def exchange(index, source, target):
        width = source.shape[1]
        copies = []
        for step, peer in enumerate(peers):
            copy = pltpu.make_async_remote_copy(
                src_ref=source.at[rows_of(peer, tokens), :],
                dst_ref=target.at[:, rows_of(head, width)],
                send_sem=x_send.at[index, step],
                recv_sem=x_recv.at[index, step],
                device_id={"head": peer},
                device_id_type=MESH,
            )
            copy.start()
            copies.append(copy)
        local = pltpu.make_async_copy(
            source.at[rows_of(head, tokens), :], target.at[:, rows_of(head, width)], local_sems.at[index]
        )
        local.start()
        waits.append((local, copies))

    copies = {}

    def push(array, kind, level, source, target, partner):
        copy = pltpu.make_async_remote_copy(
            src_ref=source,
            dst_ref=target,
            send_sem=c_send.at[array, kind, level],
            recv_sem=c_recv.at[array, kind, level],
            device_id={"ctx": partner},
            device_id_type=MESH,
        )
        copy.start()
        copies[array, kind, level] = copy

    def block(level, position):
        return rows_of((2 - level) * PLANE + position, length)

    for level in (2, 1, 0):
        for array in range(2):
            part = parts[array]
            push(array, 0, level, part.at[block(level, diagonal), :], near_buf.at[array, level, 0], base + near)
            push(array, 1, level, part.at[block(level, near), :], near_buf.at[array, level, 1], base + near)
    exchange(0, dq_ref, dq_out)
    for level in (2, 1, 0):
        for array in range(2):
            part = parts[array]
            copies[array, 0, level].wait_recv()
            far_sum[array, level] = (
                part[block(level, far), :].astype(jnp.float32) + near_buf[array, level, 0].astype(jnp.float32)
            ).astype(jnp.bfloat16)
            push(array, 2, level, far_sum.at[array, level], far_buf.at[array, level], base + far)
    for level in (2, 1, 0):
        for array in range(2):
            part = parts[array]
            copies[array, 1, level].wait_recv()
            own_sum[array, level] = part[block(level, slot), :].astype(jnp.float32) + near_buf[
                array, level, 1
            ].astype(jnp.float32)
    for level in (2, 1, 0):
        for array in range(2):
            copies[array, 2, level].wait_recv()
            total = own_sum[array, level] + far_buf[array, level].astype(jnp.float32)
            if level < 2:
                copies[array, 3, level + 1].wait_recv()
                total = total + down_buf[array, level].astype(jnp.float32)
            if level > 0:
                down_src[array, level - 1] = total.astype(jnp.bfloat16)
                push(array, 3, level, down_src.at[array, level - 1], down_buf.at[array, level - 1], down)
            else:
                final[array] = total.astype(jnp.bfloat16)
                exchange(1 + array, final.at[array], (dk_out, dv_out)[array])
    for local, remote in waits:
        local.wait()
        for copy in remote:
            copy.wait()
    for copy in copies.values():
        copy.wait_send()


def reduce(grad_query, part_keys, part_values):
    heads = lax.axis_size("head")
    length, width = grad_query.shape
    head_width = part_keys.shape[1]
    tokens = length // heads
    vmem = pl.BlockSpec(memory_space=pltpu.VMEM)
    dma = pltpu.SemaphoreType.DMA
    block = (length, head_width)
    narrow = jax.ShapeDtypeStruct((tokens, head_width * heads), jnp.bfloat16)
    return pl.pallas_call(
        reduce_kernel,
        out_shape=(jax.ShapeDtypeStruct((tokens, width * heads), jnp.bfloat16), narrow, narrow),
        in_specs=[vmem] * 3,
        out_specs=(vmem,) * 3,
        scratch_shapes=[
            pltpu.VMEM((2, 3, 2) + block, jnp.bfloat16),
            pltpu.VMEM((2, 3) + block, jnp.float32),
            pltpu.VMEM((2, 3) + block, jnp.bfloat16),
            pltpu.VMEM((2, 3) + block, jnp.bfloat16),
            pltpu.VMEM((2, 2) + block, jnp.bfloat16),
            pltpu.VMEM((2, 2) + block, jnp.bfloat16),
            pltpu.VMEM((2,) + block, jnp.bfloat16),
            dma((3,)), dma((3, heads)), dma((3, heads)), dma((2, 4, 3)), dma((2, 4, 3)),
        ],
        compiler_params=pltpu.CompilerParams(
            collective_id=1, has_side_effects=True, vmem_limit_bytes=VMEM_LIMIT
        ),
    )(grad_query, part_keys, part_values)


def on_device(queries, keys, values, output_cotangent, doc_ids):
    query_rows, grad_rows, key_window, value_window = gather(queries, output_cotangent, keys, values)
    length = query_rows.shape[0]
    own_docs = lax.dynamic_slice_in_dim(doc_ids, lax.axis_index("ctx") * length, length, 0)
    bound = jnp.sum((doc_ids[:, None] < own_docs[None, :]).astype(jnp.int32), axis=0)[None]
    return reduce(*attention(query_rows, grad_rows, key_window, value_window, bound))


def solution(mesh):
    rows = P(("ctx", "head"), None)
    return jax.shard_map(
        on_device,
        mesh=mesh,
        in_specs=(rows, rows, rows, rows, P()),
        out_specs=(rows, rows, rows),
        check_vma=False,
    )
```

```python
import functools
import math

import jax
import jax.numpy as jnp
from jax import lax
from jax.experimental import pallas as pl
from jax.experimental.pallas import tpu as pltpu
from jax.sharding import PartitionSpec as P

SPAN = 8
PLANE = SPAN // 2
SLOTS = SPAN + PLANE

masked_score = -1e30
LOG2E = math.log2(math.e)
VMEM_LIMIT = 56 * 1024 * 1024
MESH = pl.DeviceIdType.MESH


def greet(partners):
    barrier = pltpu.get_barrier_semaphore()
    for partner in partners:
        pl.semaphore_signal(barrier, inc=1, device_id=partner, device_id_type=MESH)
    pl.semaphore_wait(barrier, len(partners))


def places():
    ctx, head = lax.axis_index("ctx"), lax.axis_index("head")
    count = lax.axis_size("ctx")
    slot = lax.rem(ctx, PLANE)
    base = ctx - slot
    up = lax.rem(ctx + PLANE, count)
    down = lax.rem(ctx + count - PLANE, count)
    far = lax.rem(slot + PLANE // 2, PLANE)
    near = slot + 1 - 2 * lax.rem(slot, 2)
    diagonal = lax.rem(near + PLANE // 2, PLANE)
    return ctx, head, slot, base, up, down, near, far, diagonal


def head_peers(head):
    count = lax.axis_size("head")
    return [lax.rem(head + step, count) for step in range(1, count)]


def rows_of(index, length):
    return pl.ds(pl.multiple_of(index * length, length), length)


def gather_kernel(
    query_ref, grad_ref, key_ref, value_ref, query_out, grad_out, key_out, value_out, local_sems, x_send, x_recv, c_send, c_recv
):
    ctx, head, slot, base, up, down, near, far, diagonal = places()
    peers = head_peers(head)
    tokens = key_ref.shape[0]
    length = tokens * lax.axis_size("head")
    pairs = [
        (key_ref, key_out, slot + SPAN),
        (value_ref, value_out, slot + SPAN),
        (query_ref, query_out, 0),
        (grad_ref, grad_out, 0),
    ]
    greet(
        [{"head": peer} for peer in peers]
        + [{"ctx": up}, {"ctx": down}, {"ctx": base + near}, {"ctx": base + far}]
    )
    x_copies = []
    for index, (source, target, block) in enumerate(pairs):
        width = target.shape[1]
        start = pl.multiple_of(block * length + head * tokens, tokens)
        copies = []
        for step, peer in enumerate(peers):
            copy = pltpu.make_async_remote_copy(
                src_ref=source.at[:, rows_of(peer, width)],
                dst_ref=target.at[pl.ds(start, tokens), :],
                send_sem=x_send.at[index, step],
                recv_sem=x_recv.at[index, step],
                device_id={"head": peer},
                device_id_type=MESH,
            )
            copy.start()
            copies.append(copy)
        local = pltpu.make_async_copy(
            source.at[:, rows_of(head, width)], target.at[pl.ds(start, tokens), :], local_sems.at[index]
        )
        local.start()
        x_copies.append((local, copies))

    def arrive_local(index):
        x_copies[index][0].wait()

    plane = ctx // PLANE
    last = lax.axis_size("ctx") // PLANE - 1
    order = [head] + [lax.rem(head + len(peers) + 1 - step, len(peers) + 1) for step in range(1, len(peers) + 1)]

    def copy_of(array, piece, kind, level):
        target = (key_out, value_out)[array]
        block, shift, partner = (
            (slot, 1, up), (slot, 0, base + far), (slot, 0, base + near), (far, 0, base + near)
        )[kind]
        offset = block * length + order[piece] * tokens
        source = pl.ds(pl.multiple_of((2 - level) * PLANE * length + offset, tokens), tokens)
        landing = pl.ds(pl.multiple_of((2 - level - shift) * PLANE * length + offset, tokens), tokens)
        return pltpu.make_async_remote_copy(
            src_ref=target.at[source, :],
            dst_ref=target.at[landing, :],
            send_sem=c_send.at[array, piece, kind, level],
            recv_sem=c_recv.at[array, piece, kind, level],
            device_id={"ctx": partner},
            device_id_type=MESH,
        )

    def spread(array, piece, level):
        if level < 2:
            @pl.when(plane < last)
            def _():
                copy_of(array, piece, 0, level).start()

        copy_of(array, piece, 1, level).start()
        copy_of(array, piece, 2, level).start()

    def relay(array, piece, level):
        copy_of(array, piece, 1, level).wait_recv()
        copy_of(array, piece, 3, level).start()

    pieces = range(len(order))
    for piece in pieces:
        for array in range(2):
            if piece == 0:
                arrive_local(array)
            else:
                x_copies[array][1][piece - 1].wait_recv()
            spread(array, piece, 0)
    for level in (1, 2):
        for piece in pieces:
            @pl.when(plane >= level)
            def _():
                for array in range(2):
                    copy_of(array, piece, 0, level - 1).wait_recv()
                    spread(array, piece, level)

            for array in range(2):
                if level == 1:
                    relay(array, piece, 0)
                else:
                    @pl.when(plane >= 1)
                    def _():
                        relay(array, piece, 1)

    @pl.when(plane >= 2)
    def _():
        for piece in pieces:
            for array in range(2):
                relay(array, piece, 2)

    for level in range(3):
        @pl.when(plane >= level)
        def _():
            for piece in pieces:
                for array in range(2):
                    copy_of(array, piece, 1, level).wait_send()
                    copy_of(array, piece, 2, level).wait()
                    copy_of(array, piece, 3, level).wait()
            if level < 2:
                @pl.when(plane < last)
                def _():
                    for piece in pieces:
                        for array in range(2):
                            copy_of(array, piece, 0, level).wait_send()

    for index, (local, remote) in enumerate(x_copies):
        if index >= 2:
            local.wait()
            for copy in remote:
                copy.wait_recv()
        for copy in remote:
            copy.wait_send()


def gather(queries, output_cotangent, keys, values):
    heads = lax.axis_size("head")
    tokens, width = queries.shape
    length = tokens * heads
    head_width = keys.shape[1] // heads
    vmem = pl.BlockSpec(memory_space=pltpu.VMEM)
    rows = jax.ShapeDtypeStruct((length, width // heads), jnp.bfloat16)
    window = jax.ShapeDtypeStruct((SLOTS * length, head_width), jnp.bfloat16)
    dma = pltpu.SemaphoreType.DMA
    return pl.pallas_call(
        gather_kernel,
        out_shape=(rows, rows, window, window),
        in_specs=[vmem] * 4,
        out_specs=(vmem,) * 4,
        scratch_shapes=[dma((4,)), dma((4, heads)), dma((4, heads)), dma((2, heads, 4, 3)), dma((2, heads, 4, 3))],
        compiler_params=pltpu.CompilerParams(
            collective_id=0, has_side_effects=True, vmem_limit_bytes=VMEM_LIMIT
        ),
    )(queries, output_cotangent, keys, values)


def attention_kernel(
    query_ref, grad_ref, key_ref, value_ref, doc_ref, dq_ref, dk_ref, dv_ref,
    bias_ref, key_win, value_win, key_t_ref, value_t_ref, key_sum, value_sum, *, scaling
):
    length = query_ref.shape[0]
    width = key_ref.shape[1]
    window = key_sum.shape[0]
    group_size = query_ref.shape[1] // width
    own_block = lax.axis_index("ctx")
    slot = lax.rem(own_block, PLANE)
    reach = pl.ds(pl.multiple_of(slot * length, length), window)
    first_key = (own_block - SPAN) * length
    lanes = doc_ref.shape[1]
    own_row = own_block * (length // lanes)
    query_docs = jnp.concatenate(
        [doc_ref[pl.ds(own_row + i, 1), :] for i in range(length // lanes)], axis=1
    )
    query_pos = own_block * length + lax.broadcasted_iota(jnp.int32, (lanes, length), 1)
    for i in range(window // lanes):
        row = jnp.maximum((own_block - SPAN) * (length // lanes) + i, 0)
        key_docs = jnp.broadcast_to(doc_ref[pl.ds(row, 1), :], (lanes, lanes)).T
        key_docs = jnp.concatenate([key_docs] * (length // lanes), axis=1)
        key_pos = first_key + i * lanes + lax.broadcasted_iota(jnp.int32, (lanes, length), 0)
        allowed = (key_docs == query_docs) & (key_pos <= query_pos) & (key_pos >= 0)
        bias_ref[i * lanes : (i + 1) * lanes, :] = jnp.where(allowed, 0.0, masked_score)
    present = first_key + lax.broadcasted_iota(jnp.int32, (window, width), 0) >= 0
    key_win[...] = jnp.where(present, key_ref[reach, :].astype(jnp.float32), 0.0).astype(jnp.bfloat16)
    value_win[...] = jnp.where(present, value_ref[reach, :].astype(jnp.float32), 0.0).astype(jnp.bfloat16)
    key_t_ref[...] = key_win[...].T
    value_t_ref[...] = value_win[...].T
    key_sum[...] = jnp.zeros_like(key_sum)
    value_sum[...] = jnp.zeros_like(value_sum)
    contract_last = (((1,), (1,)), ((), ()))

    @pl.loop(0, group_size)
    def _(g):
        cols = pl.ds(pl.multiple_of(g * width, width), width)
        query = query_ref[:, cols]
        grad = grad_ref[:, cols]
        scores = lax.dot_general(key_win[...], query, contract_last, preferred_element_type=jnp.float32)
        scores = scores * (scaling * LOG2E) + bias_ref[...]
        powers = jnp.exp2(scores - jnp.max(scores, axis=0, keepdims=True))
        weights = powers * (1.0 / jnp.sum(powers, axis=0, keepdims=True))
        rounded = weights.astype(jnp.bfloat16)
        out_t = jnp.dot(value_t_ref[...], rounded, preferred_element_type=jnp.float32)
        row_dot = jnp.sum(grad.astype(jnp.float32).T * out_t, axis=0, keepdims=True)
        grad_weights = lax.dot_general(value_win[...], grad, contract_last, preferred_element_type=jnp.float32)
        grad_scores = (weights * (grad_weights - row_dot)).astype(jnp.bfloat16)
        dq_t = jnp.dot(key_t_ref[...], grad_scores, preferred_element_type=jnp.float32)
        dq_ref[:, cols] = (dq_t * scaling).T.astype(jnp.bfloat16)
        key_sum[...] += jnp.dot(grad_scores, query, preferred_element_type=jnp.float32)
        value_sum[...] += jnp.dot(rounded, grad, preferred_element_type=jnp.float32)

    dk_ref[...] = jnp.zeros_like(dk_ref)
    dv_ref[...] = jnp.zeros_like(dv_ref)
    dk_ref[reach, :] = (key_sum[...] * scaling).astype(jnp.bfloat16)
    dv_ref[reach, :] = value_sum[...].astype(jnp.bfloat16)


def attention(query_rows, grad_rows, key_window, value_window, docs):
    length = query_rows.shape[0]
    width = key_window.shape[1]
    window = (SPAN + 1) * length
    vmem = pl.BlockSpec(memory_space=pltpu.VMEM)
    parts = jax.ShapeDtypeStruct(key_window.shape, jnp.bfloat16)
    return pl.pallas_call(
        functools.partial(attention_kernel, scaling=width ** (-0.5)),
        out_shape=(jax.ShapeDtypeStruct(query_rows.shape, jnp.bfloat16), parts, parts),
        in_specs=[vmem] * 5,
        out_specs=(vmem,) * 3,
        scratch_shapes=[
            pltpu.VMEM((window, length), jnp.float32),
            pltpu.VMEM((window, width), jnp.bfloat16),
            pltpu.VMEM((window, width), jnp.bfloat16),
            pltpu.VMEM((width, window), jnp.bfloat16),
            pltpu.VMEM((width, window), jnp.bfloat16),
            pltpu.VMEM((window, width), jnp.float32),
            pltpu.VMEM((window, width), jnp.float32),
        ],
        compiler_params=pltpu.CompilerParams(vmem_limit_bytes=VMEM_LIMIT),
    )(query_rows, grad_rows, key_window, value_window, docs)


def reduce_kernel(
    dq_ref, dk_ref, dv_ref, dq_out, dk_out, dv_out,
    near_buf, own_sum, far_sum, far_buf, down_src, down_buf, final,
    local_sems, x_send, x_recv, c_send, c_recv
):
    ctx, head, slot, base, up, down, near, far, diagonal = places()
    peers = head_peers(head)
    tokens = dq_out.shape[0]
    length = dq_ref.shape[0]
    parts = (dk_ref, dv_ref)
    greet(
        [{"head": peer} for peer in peers]
        + [{"ctx": up}, {"ctx": down}, {"ctx": base + near}, {"ctx": base + far}]
    )
    waits = []

    def exchange(index, source, target):
        width = source.shape[1]
        copies = []
        for step, peer in enumerate(peers):
            copy = pltpu.make_async_remote_copy(
                src_ref=source.at[rows_of(peer, tokens), :],
                dst_ref=target.at[:, rows_of(head, width)],
                send_sem=x_send.at[index, step],
                recv_sem=x_recv.at[index, step],
                device_id={"head": peer},
                device_id_type=MESH,
            )
            copy.start()
            copies.append(copy)
        local = pltpu.make_async_copy(
            source.at[rows_of(head, tokens), :], target.at[:, rows_of(head, width)], local_sems.at[index]
        )
        local.start()
        waits.append((local, copies))

    plane = ctx // PLANE
    last = lax.axis_size("ctx") // PLANE - 1
    order = peers + [head]
    pieces = range(len(order))

    def rows(level, position, piece):
        start = ((2 - level) * PLANE + position) * length + order[piece] * tokens
        return pl.ds(pl.multiple_of(start, tokens), tokens)

    def slab(piece):
        return pl.ds(pl.multiple_of(order[piece] * tokens, tokens), tokens)

    def copy_of(array, piece, kind, level):
        part = (dk_ref, dv_ref)[array]
        here = slab(piece)
        source, target, place = (
            (lambda: part.at[rows(level, diagonal, piece), :], lambda: near_buf.at[array, level, 0, here], {"ctx": base + near}),
            (lambda: part.at[rows(level, near, piece), :], lambda: near_buf.at[array, level, 1, here], {"ctx": base + near}),
            (lambda: far_sum.at[array, level, here], lambda: far_buf.at[array, level, here], {"ctx": base + far}),
            (lambda: down_src.at[array, level - 1, here], lambda: down_buf.at[array, level - 1, here], {"ctx": down}),
        )[kind]
        return pltpu.make_async_remote_copy(
            src_ref=source(),
            dst_ref=target(),
            send_sem=c_send.at[array, piece, kind, level],
            recv_sem=c_recv.at[array, piece, kind, level],
            device_id=place,
            device_id_type=MESH,
        )

    def final_copies(array, piece):
        target = (dk_out, dv_out)[array]
        width = final.shape[2]
        source = final.at[array, slab(piece), :]
        cols = rows_of(head, width)
        if piece == len(peers):
            return pltpu.make_async_copy(source, target.at[:, cols], local_sems.at[1 + array])
        return pltpu.make_async_remote_copy(
            src_ref=source,
            dst_ref=target.at[:, cols],
            send_sem=x_send.at[1 + array, piece],
            recv_sem=x_recv.at[1 + array, piece],
            device_id={"head": peers[piece]},
            device_id_type=MESH,
        )

    for level in (2, 1, 0):
        @pl.when(plane >= level)
        def _():
            for piece in pieces:
                for array in range(2):
                    copy_of(array, piece, 0, level).start()
                    copy_of(array, piece, 1, level).start()
    exchange(0, dq_ref, dq_out)
    for level in (2, 1, 0):
        @pl.when(plane >= level)
        def _():
            for piece in pieces:
                for array in range(2):
                    here = slab(piece)
                    part = parts[array]
                    copy_of(array, piece, 0, level).wait_recv()
                    far_sum[array, level, here] = (
                        part[rows(level, far, piece), :].astype(jnp.float32)
                        + near_buf[array, level, 0, here].astype(jnp.float32)
                    ).astype(jnp.bfloat16)
                    copy_of(array, piece, 2, level).start()
    for level in (2, 1, 0):
        for piece in pieces:
            for array in range(2):
                here = slab(piece)
                part = parts[array]

                @pl.when(plane >= level)
                def _():
                    copy_of(array, piece, 1, level).wait_recv()
                    copy_of(array, piece, 2, level).wait_recv()
                    own_sum[array, level, here] = (
                        part[rows(level, slot, piece), :].astype(jnp.float32)
                        + near_buf[array, level, 1, here].astype(jnp.float32)
                        + far_buf[array, level, here].astype(jnp.float32)
                    )

                if level < 2:
                    @pl.when((plane >= level) & (plane < last))
                    def _():
                        copy_of(array, piece, 3, level + 1).wait_recv()
                        own_sum[array, level, here] += down_buf[array, level, here].astype(jnp.float32)

                if level > 0:
                    @pl.when(plane >= level)
                    def _():
                        down_src[array, level - 1, here] = own_sum[array, level, here].astype(jnp.bfloat16)
                        copy_of(array, piece, 3, level).start()
                else:
                    final[array, here] = own_sum[array, level, here].astype(jnp.bfloat16)
                    final_copies(array, piece).start()
    for level in range(3):
        @pl.when(plane >= level)
        def _():
            for piece in pieces:
                for array in range(2):
                    for kind in (0, 1, 2) + ((3,) if level else ()):
                        copy_of(array, piece, kind, level).wait_send()
    for piece in pieces:
        for array in range(2):
            final_copies(array, piece).wait()
    for local, remote in waits:
        local.wait()
        for copy in remote:
            copy.wait()


def settle_kernel(dq_ref, dk_ref, dv_ref, dq_out, dk_out, dv_out, sems):
    copies = [
        pltpu.make_async_copy(source, target, sems.at[index])
        for index, (source, target) in enumerate(((dq_ref, dq_out), (dk_ref, dk_out), (dv_ref, dv_out)))
    ]
    for copy in copies:
        copy.start()
    for copy in copies:
        copy.wait()


def settle(*arrays):
    return pl.pallas_call(
        settle_kernel,
        out_shape=tuple(jax.ShapeDtypeStruct(array.shape, array.dtype) for array in arrays),
        in_specs=[pl.BlockSpec(memory_space=pltpu.VMEM)] * 3,
        out_specs=(pl.BlockSpec(memory_space=pl.ANY),) * 3,
        scratch_shapes=[pltpu.SemaphoreType.DMA((3,))],
    )(*arrays)


def reduce(grad_query, part_keys, part_values):
    heads = lax.axis_size("head")
    length, width = grad_query.shape
    head_width = part_keys.shape[1]
    tokens = length // heads
    vmem = pl.BlockSpec(memory_space=pltpu.VMEM)
    dma = pltpu.SemaphoreType.DMA
    block = (length, head_width)
    narrow = jax.ShapeDtypeStruct((tokens, head_width * heads), jnp.bfloat16)
    return pl.pallas_call(
        reduce_kernel,
        out_shape=(jax.ShapeDtypeStruct((tokens, width * heads), jnp.bfloat16), narrow, narrow),
        in_specs=[vmem] * 3,
        out_specs=(vmem,) * 3,
        scratch_shapes=[
            pltpu.VMEM((2, 3, 2) + block, jnp.bfloat16),
            pltpu.VMEM((2, 3) + block, jnp.float32),
            pltpu.VMEM((2, 3) + block, jnp.bfloat16),
            pltpu.VMEM((2, 3) + block, jnp.bfloat16),
            pltpu.VMEM((2, 2) + block, jnp.bfloat16),
            pltpu.VMEM((2, 2) + block, jnp.bfloat16),
            pltpu.VMEM((2,) + block, jnp.bfloat16),
            dma((3,)), dma((3, heads)), dma((3, heads)), dma((2, heads, 4, 3)), dma((2, heads, 4, 3)),
        ],
        compiler_params=pltpu.CompilerParams(
            collective_id=1, has_side_effects=True, vmem_limit_bytes=VMEM_LIMIT
        ),
    )(grad_query, part_keys, part_values)


def on_device(queries, keys, values, output_cotangent, doc_ids):
    query_rows, grad_rows, key_window, value_window = gather(queries, output_cotangent, keys, values)
    docs = doc_ids.reshape(-1, key_window.shape[1])
    return settle(*reduce(*attention(query_rows, grad_rows, key_window, value_window, docs)))


def solution(mesh):
    rows = P(("ctx", "head"), None)
    return jax.shard_map(
        on_device,
        mesh=mesh,
        in_specs=(rows, rows, rows, rows, P()),
        out_specs=(rows, rows, rows),
        check_vma=False,
    )
```

```python
import functools
import math

import jax
import jax.numpy as jnp
from jax import lax
from jax.experimental import pallas as pl
from jax.experimental.pallas import tpu as pltpu
from jax.sharding import PartitionSpec as P

SPAN = 8
PLANE = SPAN // 2
SLOTS = SPAN + PLANE

masked_score = -1e30
LOG2E = math.log2(math.e)
VMEM_LIMIT = 56 * 1024 * 1024
MESH = pl.DeviceIdType.MESH


def greet(partners):
    barrier = pltpu.get_barrier_semaphore()
    for partner in partners:
        pl.semaphore_signal(barrier, inc=1, device_id=partner, device_id_type=MESH)
    pl.semaphore_wait(barrier, len(partners))


def places():
    ctx, head = lax.axis_index("ctx"), lax.axis_index("head")
    count = lax.axis_size("ctx")
    slot = lax.rem(ctx, PLANE)
    base = ctx - slot
    up = lax.rem(ctx + PLANE, count)
    down = lax.rem(ctx + count - PLANE, count)
    far = lax.rem(slot + PLANE // 2, PLANE)
    near = slot + 1 - 2 * lax.rem(slot, 2)
    diagonal = lax.rem(near + PLANE // 2, PLANE)
    return ctx, head, slot, base, up, down, near, far, diagonal


def head_peers(head):
    count = lax.axis_size("head")
    return [lax.rem(head + step, count) for step in range(1, count)]


def rows_of(index, length):
    return pl.ds(pl.multiple_of(index * length, length), length)


def attention_kernel(
    query_in, grad_in, key_in, value_in, doc_ref, dq_ref, dk_ref, dv_ref,
    query_ref, grad_ref, key_ref, value_ref, bias_ref, key_win, value_win, key_t_ref, value_t_ref, key_sum, value_sum,
    local_sems, x_send, x_recv, q_send, q_recv, c_send, c_recv, *, scaling
):
    ctx, head, slot, base, up, down, near, far, diagonal = places()
    peers = head_peers(head)
    tokens = key_in.shape[0]
    length = tokens * lax.axis_size("head")
    pairs = [
        (key_in, key_ref, slot + SPAN),
        (value_in, value_ref, slot + SPAN),
        (query_in, query_ref, 0),
        (grad_in, grad_ref, 0),
    ]
    greet(
        [{"head": peer} for peer in peers]
        + [{"ctx": up}, {"ctx": down}, {"ctx": base + near}, {"ctx": base + far}]
    )
    x_copies = []
    for index, (source, target, block) in enumerate(pairs):
        width = target.shape[1]
        start = pl.multiple_of(block * length + head * tokens, tokens)
        copies = []
        for step, peer in enumerate(peers if index < 2 else []):
            copy = pltpu.make_async_remote_copy(
                src_ref=source.at[:, rows_of(peer, width)],
                dst_ref=target.at[pl.ds(start, tokens), :],
                send_sem=x_send.at[index, step],
                recv_sem=x_recv.at[index, step],
                device_id={"head": peer},
                device_id_type=MESH,
            )
            copy.start()
            copies.append(copy)
        local = pltpu.make_async_copy(
            source.at[:, rows_of(head, width)], target.at[pl.ds(start, tokens), :], local_sems.at[index]
        )
        local.start()
        x_copies.append((local, copies))

    width = key_ref.shape[1]
    group_size = query_ref.shape[1] // width
    rows_here = pl.ds(pl.multiple_of(head * tokens, tokens), tokens)

    def head_copies(g):
        copies = []
        for array, (source, target) in enumerate(((query_in, query_ref), (grad_in, grad_ref))):
            for step, peer in enumerate(peers):
                columns = pl.ds(pl.multiple_of((peer * group_size + g) * width, width), width)
                copies.append(
                    pltpu.make_async_remote_copy(
                        src_ref=source.at[:, columns],
                        dst_ref=target.at[rows_here, pl.ds(pl.multiple_of(g * width, width), width)],
                        send_sem=q_send.at[array, step, g],
                        recv_sem=q_recv.at[array, step, g],
                        device_id={"head": peer},
                        device_id_type=MESH,
                    )
                )
        return copies

    @pl.loop(0, group_size)
    def _(g):
        for copy in head_copies(g):
            copy.start()

    def arrive_local(index):
        x_copies[index][0].wait()

    plane = ctx // PLANE
    last = lax.axis_size("ctx") // PLANE - 1
    order = [head] + [lax.rem(head + len(peers) + 1 - step, len(peers) + 1) for step in range(1, len(peers) + 1)]

    def copy_of(array, piece, kind, level):
        target = (key_ref, value_ref)[array]
        block, shift, partner = (
            (slot, 1, up), (slot, 0, base + far), (slot, 0, base + near), (far, 0, base + near)
        )[kind]
        offset = block * length + order[piece] * tokens
        source = pl.ds(pl.multiple_of((2 - level) * PLANE * length + offset, tokens), tokens)
        landing = pl.ds(pl.multiple_of((2 - level - shift) * PLANE * length + offset, tokens), tokens)
        return pltpu.make_async_remote_copy(
            src_ref=target.at[source, :],
            dst_ref=target.at[landing, :],
            send_sem=c_send.at[array, piece, kind, level],
            recv_sem=c_recv.at[array, piece, kind, level],
            device_id={"ctx": partner},
            device_id_type=MESH,
        )

    def spread(array, piece, level):
        if level < 2:
            @pl.when(plane < last)
            def _():
                copy_of(array, piece, 0, level).start()

        copy_of(array, piece, 1, level).start()
        copy_of(array, piece, 2, level).start()

    def relay(array, piece, level):
        copy_of(array, piece, 1, level).wait_recv()
        copy_of(array, piece, 3, level).start()

    pieces = range(len(order))
    for piece in pieces:
        for array in range(2):
            if piece == 0:
                arrive_local(array)
            else:
                x_copies[array][1][piece - 1].wait_recv()
            spread(array, piece, 0)
    window = key_sum.shape[0]
    own_block = ctx
    reach = pl.ds(pl.multiple_of(slot * length, length), window)
    first_key = (own_block - SPAN) * length
    lanes = doc_ref.shape[1]
    own_row = own_block * (length // lanes)
    query_docs = jnp.concatenate(
        [doc_ref[pl.ds(own_row + i, 1), :] for i in range(length // lanes)], axis=1
    )
    query_pos = own_block * length + lax.broadcasted_iota(jnp.int32, (lanes, length), 1)
    for i in range(window // lanes):
        row = jnp.maximum((own_block - SPAN) * (length // lanes) + i, 0)
        key_docs = jnp.broadcast_to(doc_ref[pl.ds(row, 1), :], (lanes, lanes)).T
        key_docs = jnp.concatenate([key_docs] * (length // lanes), axis=1)
        key_pos = first_key + i * lanes + lax.broadcasted_iota(jnp.int32, (lanes, length), 0)
        allowed = (key_docs == query_docs) & (key_pos <= query_pos) & (key_pos >= 0)
        bias_ref[i * lanes : (i + 1) * lanes, :] = jnp.where(allowed, 0.0, masked_score)
    for level in (1, 2):
        for piece in pieces:
            @pl.when(plane >= level)
            def _():
                for array in range(2):
                    copy_of(array, piece, 0, level - 1).wait_recv()
                    spread(array, piece, level)

            for array in range(2):
                if level == 1:
                    relay(array, piece, 0)
                else:
                    @pl.when(plane >= 1)
                    def _():
                        relay(array, piece, 1)

    @pl.when(plane >= 2)
    def _():
        for piece in pieces:
            for array in range(2):
                relay(array, piece, 2)

    for level in range(3):
        @pl.when(plane >= level)
        def _():
            for piece in pieces:
                for array in range(2):
                    copy_of(array, piece, 2, level).wait_recv()
                    copy_of(array, piece, 3, level).wait_recv()

    for index in (2, 3):
        arrive_local(index)
    present = first_key + lax.broadcasted_iota(jnp.int32, (window, width), 0) >= 0
    key_win[...] = jnp.where(present, key_ref[reach, :].astype(jnp.float32), 0.0).astype(jnp.bfloat16)
    value_win[...] = jnp.where(present, value_ref[reach, :].astype(jnp.float32), 0.0).astype(jnp.bfloat16)
    key_t_ref[...] = key_win[...].T
    value_t_ref[...] = value_win[...].T
    key_sum[...] = jnp.zeros_like(key_sum)
    value_sum[...] = jnp.zeros_like(value_sum)
    contract_last = (((1,), (1,)), ((), ()))

    @pl.loop(0, group_size)
    def _(g):
        for copy in head_copies(g):
            copy.wait_recv()
        cols = pl.ds(pl.multiple_of(g * width, width), width)
        query = query_ref[:, cols]
        grad = grad_ref[:, cols]
        scores = lax.dot_general(key_win[...], query, contract_last, preferred_element_type=jnp.float32)
        scores = scores * (scaling * LOG2E) + bias_ref[...]
        powers = jnp.exp2(scores - jnp.max(scores, axis=0, keepdims=True))
        weights = powers * (1.0 / jnp.sum(powers, axis=0, keepdims=True))
        rounded = weights.astype(jnp.bfloat16)
        out_t = jnp.dot(value_t_ref[...], rounded, preferred_element_type=jnp.float32)
        row_dot = jnp.sum(grad.astype(jnp.float32).T * out_t, axis=0, keepdims=True)
        grad_weights = lax.dot_general(value_win[...], grad, contract_last, preferred_element_type=jnp.float32)
        grad_scores = (weights * (grad_weights - row_dot)).astype(jnp.bfloat16)
        dq_t = jnp.dot(key_t_ref[...], grad_scores, preferred_element_type=jnp.float32)
        dq_ref[:, cols] = (dq_t * scaling).T.astype(jnp.bfloat16)
        key_sum[...] += jnp.dot(grad_scores, query, preferred_element_type=jnp.float32)
        value_sum[...] += jnp.dot(rounded, grad, preferred_element_type=jnp.float32)

    dk_ref[...] = jnp.zeros_like(dk_ref)
    dv_ref[...] = jnp.zeros_like(dv_ref)
    dk_ref[reach, :] = (key_sum[...] * scaling).astype(jnp.bfloat16)
    dv_ref[reach, :] = value_sum[...].astype(jnp.bfloat16)

    for level in range(3):
        @pl.when(plane >= level)
        def _():
            for piece in pieces:
                for array in range(2):
                    copy_of(array, piece, 1, level).wait_send()
                    copy_of(array, piece, 2, level).wait_send()
                    copy_of(array, piece, 3, level).wait_send()
            if level < 2:
                @pl.when(plane < last)
                def _():
                    for piece in pieces:
                        for array in range(2):
                            copy_of(array, piece, 0, level).wait_send()

    for _, remote in x_copies:
        for copy in remote:
            copy.wait_send()

    @pl.loop(0, group_size)
    def _(g):
        for copy in head_copies(g):
            copy.wait_send()


def attention(queries, output_cotangent, keys, values, docs):
    heads = lax.axis_size("head")
    tokens, query_width = queries.shape
    length = tokens * heads
    width = keys.shape[1] // heads
    group_size = query_width // heads // width
    window = (SPAN + 1) * length
    vmem = pl.BlockSpec(memory_space=pltpu.VMEM)
    dma = pltpu.SemaphoreType.DMA
    rows = (length, query_width // heads)
    parts = jax.ShapeDtypeStruct((SLOTS * length, width), jnp.bfloat16)
    return pl.pallas_call(
        functools.partial(attention_kernel, scaling=width ** (-0.5)),
        out_shape=(jax.ShapeDtypeStruct(rows, jnp.bfloat16), parts, parts),
        in_specs=[vmem] * 5,
        out_specs=(vmem,) * 3,
        scratch_shapes=[
            pltpu.VMEM(rows, jnp.bfloat16),
            pltpu.VMEM(rows, jnp.bfloat16),
            pltpu.VMEM((SLOTS * length, width), jnp.bfloat16),
            pltpu.VMEM((SLOTS * length, width), jnp.bfloat16),
            pltpu.VMEM((window, length), jnp.float32),
            pltpu.VMEM((window, width), jnp.bfloat16),
            pltpu.VMEM((window, width), jnp.bfloat16),
            pltpu.VMEM((width, window), jnp.bfloat16),
            pltpu.VMEM((width, window), jnp.bfloat16),
            pltpu.VMEM((window, width), jnp.float32),
            pltpu.VMEM((window, width), jnp.float32),
            dma((4,)), dma((2, heads)), dma((2, heads)),
            dma((2, heads, group_size)), dma((2, heads, group_size)),
            dma((2, heads, 4, 3)), dma((2, heads, 4, 3)),
        ],
        compiler_params=pltpu.CompilerParams(
            collective_id=0, has_side_effects=True, vmem_limit_bytes=VMEM_LIMIT
        ),
    )(queries, output_cotangent, keys, values, docs)


def reduce_kernel(
    dq_ref, dk_ref, dv_ref, dq_out, dk_out, dv_out,
    near_buf, own_sum, far_sum, far_buf, down_src, down_buf, final,
    local_sems, x_send, x_recv, c_send, c_recv
):
    ctx, head, slot, base, up, down, near, far, diagonal = places()
    peers = head_peers(head)
    tokens = dq_out.shape[0]
    length = dq_ref.shape[0]
    parts = (dk_ref, dv_ref)
    greet(
        [{"head": peer} for peer in peers]
        + [{"ctx": up}, {"ctx": down}, {"ctx": base + near}, {"ctx": base + far}]
    )
    waits = []

    def exchange(index, source, target):
        width = source.shape[1]
        copies = []
        for step, peer in enumerate(peers):
            copy = pltpu.make_async_remote_copy(
                src_ref=source.at[rows_of(peer, tokens), :],
                dst_ref=target.at[:, rows_of(head, width)],
                send_sem=x_send.at[index, step],
                recv_sem=x_recv.at[index, step],
                device_id={"head": peer},
                device_id_type=MESH,
            )
            copy.start()
            copies.append(copy)
        local = pltpu.make_async_copy(
            source.at[rows_of(head, tokens), :], target.at[:, rows_of(head, width)], local_sems.at[index]
        )
        local.start()
        waits.append((local, copies))

    plane = ctx // PLANE
    last = lax.axis_size("ctx") // PLANE - 1
    order = peers + [head]
    pieces = range(len(order))

    def rows(level, position, piece):
        start = ((2 - level) * PLANE + position) * length + order[piece] * tokens
        return pl.ds(pl.multiple_of(start, tokens), tokens)

    def slab(piece):
        return pl.ds(pl.multiple_of(order[piece] * tokens, tokens), tokens)

    def copy_of(array, piece, kind, level):
        part = (dk_ref, dv_ref)[array]
        here = slab(piece)
        source, target, place = (
            (lambda: part.at[rows(level, diagonal, piece), :], lambda: near_buf.at[array, level, 0, here], {"ctx": base + near}),
            (lambda: part.at[rows(level, near, piece), :], lambda: near_buf.at[array, level, 1, here], {"ctx": base + near}),
            (lambda: far_sum.at[array, level, here], lambda: far_buf.at[array, level, here], {"ctx": base + far}),
            (lambda: down_src.at[array, level - 1, here], lambda: down_buf.at[array, level - 1, here], {"ctx": down}),
        )[kind]
        return pltpu.make_async_remote_copy(
            src_ref=source(),
            dst_ref=target(),
            send_sem=c_send.at[array, piece, kind, level],
            recv_sem=c_recv.at[array, piece, kind, level],
            device_id=place,
            device_id_type=MESH,
        )

    def final_copies(array, piece):
        target = (dk_out, dv_out)[array]
        width = final.shape[2]
        source = final.at[array, slab(piece), :]
        cols = rows_of(head, width)
        if piece == len(peers):
            return pltpu.make_async_copy(source, target.at[:, cols], local_sems.at[1 + array])
        return pltpu.make_async_remote_copy(
            src_ref=source,
            dst_ref=target.at[:, cols],
            send_sem=x_send.at[1 + array, piece],
            recv_sem=x_recv.at[1 + array, piece],
            device_id={"head": peers[piece]},
            device_id_type=MESH,
        )

    for level in (2, 1, 0):
        @pl.when(plane >= level)
        def _():
            for piece in pieces:
                for array in range(2):
                    copy_of(array, piece, 0, level).start()
                    copy_of(array, piece, 1, level).start()
    exchange(0, dq_ref, dq_out)
    for level in (2, 1, 0):
        @pl.when(plane >= level)
        def _():
            for piece in pieces:
                for array in range(2):
                    here = slab(piece)
                    part = parts[array]
                    copy_of(array, piece, 0, level).wait_recv()
                    far_sum[array, level, here] = (
                        part[rows(level, far, piece), :].astype(jnp.float32)
                        + near_buf[array, level, 0, here].astype(jnp.float32)
                    ).astype(jnp.bfloat16)
                    copy_of(array, piece, 2, level).start()
    for level in (2, 1, 0):
        for piece in pieces:
            for array in range(2):
                here = slab(piece)
                part = parts[array]

                @pl.when(plane >= level)
                def _():
                    copy_of(array, piece, 1, level).wait_recv()
                    copy_of(array, piece, 2, level).wait_recv()
                    own_sum[array, level, here] = (
                        part[rows(level, slot, piece), :].astype(jnp.float32)
                        + near_buf[array, level, 1, here].astype(jnp.float32)
                        + far_buf[array, level, here].astype(jnp.float32)
                    )

                if level < 2:
                    @pl.when((plane >= level) & (plane < last))
                    def _():
                        copy_of(array, piece, 3, level + 1).wait_recv()
                        own_sum[array, level, here] += down_buf[array, level, here].astype(jnp.float32)

                if level > 0:
                    @pl.when(plane >= level)
                    def _():
                        down_src[array, level - 1, here] = own_sum[array, level, here].astype(jnp.bfloat16)
                        copy_of(array, piece, 3, level).start()
                else:
                    final[array, here] = own_sum[array, level, here].astype(jnp.bfloat16)
                    final_copies(array, piece).start()
    for level in range(3):
        @pl.when(plane >= level)
        def _():
            for piece in pieces:
                for array in range(2):
                    for kind in (0, 1, 2) + ((3,) if level else ()):
                        copy_of(array, piece, kind, level).wait_send()
    for piece in pieces:
        for array in range(2):
            final_copies(array, piece).wait()
    for local, remote in waits:
        local.wait()
        for copy in remote:
            copy.wait()


def settle_kernel(dq_ref, dk_ref, dv_ref, dq_out, dk_out, dv_out, sems):
    copies = [
        pltpu.make_async_copy(source, target, sems.at[index])
        for index, (source, target) in enumerate(((dq_ref, dq_out), (dk_ref, dk_out), (dv_ref, dv_out)))
    ]
    for copy in copies:
        copy.start()
    for copy in copies:
        copy.wait()


def settle(*arrays):
    return pl.pallas_call(
        settle_kernel,
        out_shape=tuple(jax.ShapeDtypeStruct(array.shape, array.dtype) for array in arrays),
        in_specs=[pl.BlockSpec(memory_space=pltpu.VMEM)] * 3,
        out_specs=(pl.BlockSpec(memory_space=pl.ANY),) * 3,
        scratch_shapes=[pltpu.SemaphoreType.DMA((3,))],
    )(*arrays)


def reduce(grad_query, part_keys, part_values):
    heads = lax.axis_size("head")
    length, width = grad_query.shape
    head_width = part_keys.shape[1]
    tokens = length // heads
    vmem = pl.BlockSpec(memory_space=pltpu.VMEM)
    dma = pltpu.SemaphoreType.DMA
    block = (length, head_width)
    narrow = jax.ShapeDtypeStruct((tokens, head_width * heads), jnp.bfloat16)
    return pl.pallas_call(
        reduce_kernel,
        out_shape=(jax.ShapeDtypeStruct((tokens, width * heads), jnp.bfloat16), narrow, narrow),
        in_specs=[vmem] * 3,
        out_specs=(vmem,) * 3,
        scratch_shapes=[
            pltpu.VMEM((2, 3, 2) + block, jnp.bfloat16),
            pltpu.VMEM((2, 3) + block, jnp.float32),
            pltpu.VMEM((2, 3) + block, jnp.bfloat16),
            pltpu.VMEM((2, 3) + block, jnp.bfloat16),
            pltpu.VMEM((2, 2) + block, jnp.bfloat16),
            pltpu.VMEM((2, 2) + block, jnp.bfloat16),
            pltpu.VMEM((2,) + block, jnp.bfloat16),
            dma((3,)), dma((3, heads)), dma((3, heads)), dma((2, heads, 4, 3)), dma((2, heads, 4, 3)),
        ],
        compiler_params=pltpu.CompilerParams(
            collective_id=1, has_side_effects=True, vmem_limit_bytes=VMEM_LIMIT
        ),
    )(grad_query, part_keys, part_values)


def on_device(queries, keys, values, output_cotangent, doc_ids):
    docs = doc_ids.reshape(-1, keys.shape[1] // lax.axis_size("head"))
    return settle(*reduce(*attention(queries, output_cotangent, keys, values, docs)))


def solution(mesh):
    rows = P(("ctx", "head"), None)
    return jax.shard_map(
        on_device,
        mesh=mesh,
        in_specs=(rows, rows, rows, rows, P()),
        out_specs=(rows, rows, rows),
        check_vma=False,
    )
```
